32 devices in a mesh: tm: 2 (over y), obs: 16 (over z, x, core).
Axes of the slice: x: 2, y: 2, z: 4, core: 2. Of those that a mesh axis runs over, the one named last changes fastest.
Arguments:
- flux: bfloat16 [4, 64, 16384], P('tm', 'obs'), may hold values from -6 to 6
- footprint: bfloat16 [2048, 16384], P(('tm', 'obs')), may hold values from -0.046875 to 0.046875
- entry_owner: int32 [2048, 1], P(('tm', 'obs')), may hold values from 0 to 15; in each aligned block of 64 rows (0 to 63, 64 to 127, ...) at most 8 rows name the same one
- entry_tile: int32 [32, 64], P(('tm', 'obs')), may hold values from 0 to 3
- entry_lag: int32 [32, 64], P(('tm', 'obs')), may hold values from 0 to 1
- entry_sounding: int32 [32, 64], P(('tm', 'obs')), may hold values from 0 to 15, never falling along the last dimension, each value on 1 to 8 neighbouring positions
- sounding_window: int32 [32, 16], P(('tm', 'obs')), may hold values from 1 to 3
- observed: float32 [32, 16], P(('tm', 'obs')), may hold values from -8 to 8
- obs_weight: float32 [32, 16], P(('tm', 'obs')), may hold values from 0.25 to 4
Outputs:
- modeled: float32 [32, 16], P(('tm', 'obs'))
- gradient: float32 [4, 64, 16384], P('tm', 'obs')
The draws below stay inside these ranges and needn't reach their ends.
Inputs may be any that keep to these rules, and one draw needn't show every extreme that they name: `entry_owner`: among the 64 entries of one device no owner is named more than 8 times, and on some device some owner is named exactly 8 times.
All inputs are finite; a program needn't handle non-finite values.
Results may differ from the reference program's by a relative error of at most 0.0029.
Values may be sent and summed in bfloat16 or wider, within the bound.
A program may use at most 64 MiB of HBM per device.

```python
import math
import jax
import jax.numpy as jnp
import numpy as np
from jax import lax

CELLS = 16384
E_DEV = 64
TILE_DEV = 4
S_DEV = 16
WIN = 4
TILES = 64
LAGS = 2
CAP = 8
N_OBS = 16
DEVICES = 32


def plant(result, own_key, smallest, top_value):
    place = [jax.random.randint(jax.random.fold_in(own_key, axis), (), 0, length) for axis, length in enumerate(result.shape)]
    main_axis = result.shape.index(max(result.shape))
    beside = place[:main_axis] + [(place[main_axis] + 1) % result.shape[main_axis]] + place[main_axis + 1:]
    return result.at[tuple(place)].set(smallest).at[tuple(beside)].set(top_value)


def shard_levels(key, shape, cuts, low, largest):
    factor_of = 1.0
    for axis_at, parts in cuts:
        heights = jax.random.uniform(jax.random.fold_in(jax.random.fold_in(key, 6), axis_at), (parts,), jnp.float32, low / len(cuts), largest / len(cuts))
        factor_of = factor_of * jnp.repeat(jnp.exp(heights), shape[axis_at] // parts).reshape((-1,) + (1,) * (len(shape) - 1 - axis_at))
    return factor_of


def split_up(count, total, limit, lean):
    loads = [(1 << 20) // math.isqrt(grade ** lean) + 1 for grade in range(2, count + 1)]
    rest, counts = total - limit - (count - 1), [1] * (count - 1)
    while rest > 0:
        candidates = [i for i in range(count - 1) if counts[i] < limit]
        mass, remaining = sum([loads[i] for i in candidates]), rest
        for i in candidates:
            extra = min(limit - counts[i], max(1, remaining * loads[i] // mass), rest)
            counts[i] = counts[i] + extra
            rest = rest - extra
    return np.array([limit] + counts)


def ragged_sizes(stream_key, count, total, most, slope):
    if count == 2:
        one = jax.random.randint(stream_key, (), max(1, total - most), min(most, total - 1) + 1)
        return jnp.stack([one, total - one])
    lengths = jnp.asarray(split_up(count, total, most, slope), jnp.int32)
    couples = (count - 1) // 2
    giver, receiver = lengths[1:1 + 2 * couples:2], lengths[2:2 + 2 * couples:2]
    room = jnp.minimum(giver - 1, most - receiver)
    moved = jax.random.randint(jax.random.fold_in(stream_key, 1), (couples,), 0, 1 << 20) % (room + 1)
    lengths = lengths.at[1:1 + 2 * couples:2].set(giver - moved).at[2:2 + 2 * couples:2].set(receiver + moved)
    return lengths[jax.random.permutation(jax.random.fold_in(stream_key, 2), count)]


def routed_block(key, own, number, rows, amount, top, most, lean):
    order = jax.random.permutation(key, amount)
    crowded, common = shares(amount, rows * top, most, lean, True), shares(amount, rows * top, most, lean, False)
    places = jnp.arange(amount)

    def named(sizes, offset_by):
        used = int((sizes > 0).sum())
        fixed = max(1, used // 4)
        shifted = fixed + (places - fixed + offset_by * (used - fixed)) % max(1, amount - fixed)
        return jnp.zeros((amount,), jnp.int32).at[order[jnp.where(places < fixed, places, shifted)]].set(jnp.asarray(sizes, jnp.int32))

    sizes = jnp.where(number % 4 == 0, named(crowded, number // 4), named(common, number - number // 4 - 1))
    mixed = jax.random.permutation(jax.random.fold_in(own, 3), amount)
    donor, taker = mixed[0:amount // 2 * 2:2], mixed[1:amount // 2 * 2:2]
    margin = jnp.minimum(sizes[donor] - 1, most - sizes[taker]) // 2
    margin = jnp.where((donor == order[0]) | (taker == order[0]) | (sizes[taker] == 0), 0, jnp.maximum(margin, 0))
    shifted = jax.random.randint(jax.random.fold_in(own, 4), (amount // 2,), 0, 1 << 20) % (margin + 1)
    sizes = sizes.at[donor].add(-shifted).at[taker].add(shifted)
    labels = jnp.searchsorted(jnp.cumsum(sizes), jnp.arange(rows * top), side="right").astype(jnp.int32)
    table = labels.reshape(top, rows).T
    table = table[jax.random.permutation(jax.random.fold_in(own, 1), rows)]
    offset_by = jax.random.randint(jax.random.fold_in(own, 2), (rows, 1), 0, top)
    return jnp.take_along_axis(table, (jnp.arange(top)[None, :] + offset_by) % top, axis=1)


def shares(count, total, limit, slope, full):
    loads = [(1 << 20) // math.isqrt(grade ** slope) + 1 for grade in range(1, count + 1)]
    largest = limit if full else min(limit, max(-(-total // count), total * loads[0] // sum(loads)))
    least = 1 if total - largest >= count - 1 else 0
    given, rest = [largest] + [least] * (count - 1), total - largest - least * (count - 1)
    while rest > 0:
        candidates = [i for i in range(1, count) if given[i] < largest] or [i for i in range(1, count) if given[i] < limit]
        pool, left = sum([loads[i] for i in candidates]), rest
        for i in candidates:
            extra = min(limit - given[i], max(1, left * loads[i] // pool), rest)
            given[i] = given[i] + extra
            rest = rest - extra
    return np.array(given)


def gaussian(rng, shape, scale, most, pieces=(), kind=jnp.bfloat16):
    drawn = scale * jax.random.normal(rng, shape, jnp.float32)
    if pieces:
        drawn = drawn * shard_levels(rng, shape, pieces, -0.22, 0.18)
    return jnp.clip(drawn, -most, most).astype(kind)


def setup_inputs(seed: int = 0) -> dict:
    arg_keys = jax.random.split(jax.random.key(seed), 10)
    flux = gaussian(arg_keys[0], (WIN, TILES, CELLS), 1.0, 6.0, ((0, 2), (1, 16)))
    footprint = gaussian(arg_keys[1], (DEVICES * E_DEV, CELLS), CELLS ** -0.5, 0.046875, ((0, 32),))
    entry_owner_keys = jax.random.split(jax.random.fold_in(arg_keys[2], 1), (DEVICES * E_DEV) // E_DEV)
    entry_owner_turns = jax.random.permutation(jax.random.fold_in(arg_keys[2], 3), (DEVICES * E_DEV) // E_DEV)
    entry_owner = jax.vmap(lambda own, number: routed_block(jax.random.fold_in(arg_keys[2], 2), own, number, E_DEV, N_OBS, 1, CAP, 2))(entry_owner_keys, entry_owner_turns).reshape((DEVICES * E_DEV, 1))
    entry_tile = plant(jax.random.randint(arg_keys[3], (DEVICES, E_DEV), 0, TILE_DEV), jax.random.fold_in(arg_keys[3], 1), 0, TILE_DEV - 1).astype(jnp.int32)
    entry_lag = plant(jax.random.randint(arg_keys[4], (DEVICES, E_DEV), 0, LAGS), jax.random.fold_in(arg_keys[4], 1), 0, LAGS - 1).astype(jnp.int32)
    entry_sounding = jax.vmap(lambda own: jnp.searchsorted(jnp.cumsum(ragged_sizes(own, S_DEV, E_DEV, 8, 1)), jnp.arange(E_DEV), side="right"))(jax.random.split(arg_keys[5], DEVICES)).reshape((DEVICES, E_DEV)).astype(jnp.int32)
    sounding_window = plant(jax.random.randint(arg_keys[6], (DEVICES, S_DEV), LAGS - 1, WIN), jax.random.fold_in(arg_keys[6], 1), LAGS - 1, WIN - 1).astype(jnp.int32)
    observed = gaussian(arg_keys[7], (DEVICES, S_DEV), 2.0, 8.0, ((0, 32),), jnp.float32)
    obs_weight = jnp.clip(jnp.exp(math.log(4.0) - 2.7725887 * jax.random.uniform(arg_keys[8], (DEVICES, S_DEV), jnp.float32) ** shard_levels(arg_keys[8], (DEVICES, S_DEV), ((0, 32),), -0.2, 0.2)), 0.25, 4.0)
    return {"flux": flux, "footprint": footprint, "entry_owner": entry_owner, "entry_tile": entry_tile, "entry_lag": entry_lag, "entry_sounding": entry_sounding, "sounding_window": sounding_window, "observed": observed, "obs_weight": obs_weight}


def reference(flux, footprint, entry_owner, entry_tile, entry_lag, entry_sounding, sounding_window, observed, obs_weight):
    flat_flux = flux.reshape(WIN * TILES, CELLS)
    blocks = footprint.reshape(DEVICES, E_DEV, CELLS)
    owners = entry_owner.reshape(DEVICES, E_DEV)
    window = jnp.take_along_axis(sounding_window, entry_sounding, axis=1) - entry_lag
    row_ids = (window * TILES + owners * TILE_DEV + entry_tile).astype(jnp.int32)

    def forward(inputs):
        block_rows, row_index = inputs
        selected = flat_flux[row_index]
        return jnp.sum(block_rows.astype(jnp.float32) * selected.astype(jnp.float32), axis=1)

    entry_dots = lax.map(forward, (blocks, row_ids))
    onehot = (entry_sounding[:, :, None] == jnp.arange(S_DEV, dtype=jnp.int32)[None, None, :]).astype(jnp.float32)
    modeled = jnp.sum(entry_dots[:, :, None] * onehot, axis=1)
    residual = obs_weight * (modeled - observed)
    entry_resid = jnp.take_along_axis(residual, entry_sounding, axis=1)

    def accumulate(running, inputs):
        block_rows, row_index, resid_rows = inputs
        contribution = (resid_rows[:, None] * block_rows.astype(jnp.float32)).astype(jnp.bfloat16).astype(jnp.float32)
        return running.at[row_index].add(contribution), None

    gradient, _ = lax.scan(accumulate, jnp.zeros((WIN * TILES, CELLS), jnp.float32), (blocks, row_ids, entry_resid))
    return modeled, gradient.reshape(WIN, TILES, CELLS)
```

```python
import functools

import jax
import jax.numpy as jnp
from jax import lax
from jax.experimental import pallas as pl
from jax.experimental.pallas import tpu as pltpu
from jax.sharding import PartitionSpec as P


def per_device(
    flux,
    footprint,
    entry_owner,
    entry_tile,
    entry_lag,
    entry_sounding,
    sounding_window,
    observed,
    obs_weight,
):
    peer_count = lax.axis_size("obs")
    entry_count = footprint.shape[0]
    cell_count = footprint.shape[1]
    tile_dev = flux.shape[1]
    sounding_count = observed.shape[1]
    slot_cap = 2 * entry_count // peer_count
    owners = entry_owner[:, 0]
    sounding = entry_sounding[0]
    sounding_hot = sounding[:, None] == jnp.arange(sounding_count, dtype=jnp.int32)[None, :]
    window = jnp.sum(jnp.where(sounding_hot, sounding_window[0][None, :], 0), axis=1) - entry_lag[0]
    target = window * tile_dev + entry_tile[0]
    owner_hot = (owners[:, None] == jnp.arange(peer_count, dtype=jnp.int32)[None, :]).astype(
        jnp.int32
    )
    rank_within = jnp.sum((jnp.cumsum(owner_hot, axis=0) - owner_hot) * owner_hot, axis=1)
    slot_index = owners * slot_cap + rank_within
    send_blocks = (
        jnp.zeros((peer_count * slot_cap, cell_count), jnp.bfloat16).at[slot_index].set(footprint)
    )
    send_blocks = send_blocks.reshape(peer_count, slot_cap, cell_count)
    send_target = jnp.zeros((peer_count * slot_cap,), jnp.int32).at[slot_index].set(target)
    send_target = send_target.reshape(peer_count, slot_cap)
    everything = lax.all_gather(flux, "tm", axis=0, tiled=True).reshape(-1, cell_count)
    got_blocks, got_target = (
        lax.all_to_all(send_blocks, "obs", split_axis=0, concat_axis=0, tiled=True),
        lax.all_to_all(send_target, "obs", split_axis=0, concat_axis=0, tiled=True),
    )
    selected = everything[got_target.reshape(-1)].reshape(got_blocks.shape)
    returned = lax.all_to_all(
        jnp.einsum("pkc,pkc->pk", got_blocks, selected, preferred_element_type=jnp.float32),
        "obs",
        split_axis=0,
        concat_axis=0,
        tiled=True,
    )
    entry_dots = returned.reshape(-1)[slot_index]
    modeled = jnp.sum(jnp.where(sounding_hot, entry_dots[:, None], 0.0), axis=0)
    residual = obs_weight[0] * (modeled - observed[0])
    entry_resid = jnp.sum(jnp.where(sounding_hot, residual[None, :], 0.0), axis=1)
    slot_resid = jnp.zeros((peer_count * slot_cap,), jnp.float32).at[slot_index].set(entry_resid)
    got_resid = lax.all_to_all(
        slot_resid.reshape(peer_count, slot_cap), "obs", split_axis=0, concat_axis=0, tiled=True
    )
    contribution = (got_resid[:, :, None] * got_blocks).astype(jnp.bfloat16)
    targets = got_target
    contribution = contribution.reshape(-1, cell_count)
    targets = targets.reshape(-1)
    row_count = flux.shape[0] * lax.axis_size("tm")
    row_ids = jnp.arange(row_count * tile_dev, dtype=jnp.int32)
    row_match = (row_ids[:, None] == targets[None, :]).astype(jnp.bfloat16)
    summed = jnp.dot(row_match, contribution, preferred_element_type=jnp.float32)
    gradient = lax.psum_scatter(
        summed.reshape(row_count, tile_dev * cell_count), "tm", scatter_dimension=0, tiled=True
    )
    gradient = gradient.reshape(flux.shape[0], tile_dev, cell_count)
    return (modeled[None, :], gradient)


CHUNKS = 8


def eye(n):
    return lax.broadcasted_iota(jnp.int32, (n, n), 0) == lax.broadcasted_iota(jnp.int32, (n, n), 1)


def to_col(row):
    return jnp.sum(jnp.where(eye(row.shape[1]), row, 0.0), axis=1, keepdims=True)


def to_row(col):
    return jnp.sum(jnp.where(eye(col.shape[0]), col, 0.0), axis=0, keepdims=True)


def plane_kernel(
    depth, windows, tile_dev, flux, foot, owner, tile, lag, sounding, swin, observed, weight,
    modeled_out, out,
    staged, gath, foot_all, meta_all, val_all, pick, contrib, part, send_up, send_dn, recv_up, recv_dn, total,
    flux_s, flux_r, meta_s, meta_r, foot_s, foot_r, zup_s, zup_r, zdn_s, zdn_r, val_s, val_r,
    gup_s, gup_r, gdn_s, gdn_r, out_s, out_r, local_sem,
):
    entries, all_cells = foot.shape
    cells = all_cells // 8
    rows_dev = windows * tile_dev
    rows_plane = 8 * rows_dev
    rows_all = depth * rows_plane
    sounds = observed.shape[1]
    pair = 2 * entries
    chunk = cells // CHUNKS
    y = lax.axis_index("tm")
    o = lax.axis_index("obs")
    core = lax.rem(o, 2)
    x = lax.rem(o // 2, 2)
    z = o // 4
    chip = y * 2 + x
    me = chip * 2 + core
    has_up = z < depth - 1
    has_down = z > 0
    above = (y, o + 4)
    below = (y, o - 4)

    def peer(k):
        yy = 1 - y if k & 4 else y
        xx = 1 - x if k & 2 else x
        cc = 1 - core if k & 1 else core
        return yy, xx, cc

    def device(k):
        yy, xx, cc = peer(k)
        return (yy, z * 4 + xx * 2 + cc)

    def place_of(k):
        yy, xx, cc = peer(k)
        return (yy * 2 + xx) * 2 + cc

    def chip_of(q):
        yy, xx, _ = peer(2 * q)
        return yy * 2 + xx

    def eighth(k):
        return pl.ds(pl.multiple_of(place_of(k) * cells, cells), cells)

    def remote(src, dst, send, recv, to):
        return pltpu.make_async_remote_copy(
            src_ref=src, dst_ref=dst, send_sem=send, recv_sem=recv,
            device_id=to, device_id_type=pl.DeviceIdType.MESH,
        )

    barrier = pltpu.get_barrier_semaphore()

    def greet(to):
        pl.semaphore_signal(barrier, inc=1, device_id=to, device_id_type=pl.DeviceIdType.MESH)

    for k in range(1, 8):
        greet(device(k))
    pl.when(has_up)(lambda: greet(above))
    pl.when(has_down)(lambda: greet(below))
    own_flux = pltpu.make_async_copy(flux.at[:, :, eighth(0)], staged.at[z, chip, core], local_sem.at[0])
    own_foot = pltpu.make_async_copy(
        foot.at[:, eighth(0)], foot_all.at[pl.ds(pl.multiple_of(me * entries, entries), entries)], local_sem.at[1]
    )
    own_flux.start()
    own_foot.start()

    hot = lax.broadcasted_iota(jnp.int32, (sounds, entries), 0) == sounding[...]
    window = jnp.sum(
        jnp.where(hot, to_col(swin[...].astype(jnp.float32)), 0.0), axis=0, keepdims=True
    ).astype(jnp.int32) - lag[...]
    own = owner[...]
    late = jnp.where(window >= windows, 1, 0)
    holder = ((own >> 2) * 4 + late * 2 + ((own >> 1) & 1)) * 2 + (own & 1)
    ids = holder * rows_dev + (window - late * windows) * tile_dev + tile[...]
    base = jnp.zeros((1, entries), jnp.float32)
    fill = jnp.zeros((1, pair - sounds), jnp.float32)
    meta_all[me] = jnp.concatenate(
        [
            jnp.concatenate([ids.astype(jnp.float32), base], axis=1),
            jnp.concatenate([(sounding[...] + core * sounds).astype(jnp.float32), base], axis=1),
            jnp.concatenate([observed[...], fill], axis=1),
            jnp.concatenate([weight[...], fill], axis=1),
            jnp.zeros((4, pair), jnp.float32),
        ],
        axis=0,
    )
    pl.semaphore_wait(barrier, 7 + jnp.where(has_up, 1, 0) + jnp.where(has_down, 1, 0))

    def flux_copy(k):
        return remote(
            flux.at[:, :, eighth(k)], staged.at[z, chip, core], flux_s.at[k], flux_r.at[k], device(k)
        )

    def meta_copy(k):
        return remote(meta_all.at[me], meta_all.at[me], meta_s.at[k], meta_r.at[k], device(k))

    def foot_copy(k):
        into = foot_all.at[pl.ds(pl.multiple_of(me * entries, entries), entries)]
        return remote(foot.at[:, eighth(k)], into, foot_s.at[k], foot_r.at[k], device(k))

    def val_copy(k):
        return remote(val_all.at[me], val_all.at[me], val_s.at[k], val_r.at[k], device(k))

    def z_up(zz, q):
        block = staged.at[zz, chip_of(q)]
        return remote(block, block, zup_s.at[zz, q], zup_r.at[zz, q], above)

    def z_dn(zz, q):
        block = staged.at[zz, chip_of(q)]
        return remote(block, block, zdn_s.at[zz, q], zdn_r.at[zz, q], below)

    for k in range(1, 8):
        flux_copy(k).start()
    for k in (6, 7, 2, 4, 3, 5, 1):
        if k == 6:
            for j in range(1, 8):
                meta_copy(j).start()
        foot_copy(k).start()

    def settle(zz, q):
        at = chip_of(q)
        rows = pl.ds(pl.multiple_of(zz * rows_plane + at * 2 * rows_dev, 2 * rows_dev), 2 * rows_dev)

        def body(step, carry):
            span = pl.ds(pl.multiple_of(step * 512, 512), 512)
            gath[rows, span] = staged[zz, at, :, :, :, span].reshape(2 * rows_dev, 512)
            return carry

        lax.fori_loop(0, cells // 512, body, 0)

    for q in range(4):
        if q == 0:
            own_flux.wait()
        else:
            flux_copy(2 * q).wait_recv()
        flux_copy(2 * q + 1).wait_recv()
        pl.when(has_up)(lambda: z_up(z, q).start())
        pl.when(has_down)(lambda: z_dn(z, q).start())
        settle(z, q)
    for s in range(1, depth):
        for q in range(4):
            @pl.when(z >= s)
            def _():
                z_up(z - s, q).wait_recv()
                pl.when(has_up)(lambda: z_up(z - s, q).start())
                settle(z - s, q)

            @pl.when(z + s < depth)
            def _():
                z_dn(z + s, q).wait_recv()
                pl.when(has_down)(lambda: z_dn(z + s, q).start())
                settle(z + s, q)

    for k in range(1, 8):
        meta_copy(k).wait_recv()
    id_rows, hots, obs_cols, wgt_cols = [], [], [], []
    for q in range(4):
        first, second = meta_all[2 * q], meta_all[2 * q + 1]
        both = [jnp.concatenate([first[r : r + 1, :entries], second[r : r + 1, :entries]], axis=1) for r in (0, 1)]
        id_rows.append(both[0].astype(jnp.int32))
        hots.append(
            lax.broadcasted_iota(jnp.int32, (2 * sounds, pair), 0) == both[1].astype(jnp.int32)
        )
        obs_cols.append(
            to_col(jnp.concatenate([first[2:3, :sounds], second[2:3, :sounds]], axis=1))
        )
        wgt_cols.append(
            to_col(jnp.concatenate([first[3:4, :sounds], second[3:4, :sounds]], axis=1))
        )
        row_at = lax.broadcasted_iota(jnp.int32, (rows_all, pair), 0)
        pick[:, q * pair : (q + 1) * pair] = jnp.where(row_at == id_rows[q], 1.0, 0.0).astype(jnp.bfloat16)

    def partial_values(q):
        at = chip_of(q)
        rows = pl.ds(pl.multiple_of(at * pair, pair), pair)
        acc = lax.dot_general(
            gath[...], foot_all[rows, :], (((1,), (1,)), ((), ())), preferred_element_type=jnp.float32
        )
        first, second = meta_all[2 * at], meta_all[2 * at + 1]
        mine = jnp.concatenate([first[0:1, :entries], second[0:1, :entries]], axis=1).astype(jnp.int32)
        row_at = lax.broadcasted_iota(jnp.int32, (rows_all, pair), 0)
        val_all[me, at] = jnp.sum(jnp.where(row_at == mine, acc, 0.0), axis=0, keepdims=True)

    for q in (3, 0, 1, 2):
        if q == 0:
            own_foot.wait()
        else:
            foot_copy(2 * q).wait_recv()
        foot_copy(2 * q + 1).wait_recv()
        partial_values(q)
    for k in (6, 7, 2, 4, 3, 5, 1):
        val_copy(k).start()
    for k in (1, 2, 3, 4, 5, 6, 7):
        val_copy(k).wait_recv()
    model_cols, resids = [], []
    for q in range(4):
        value = val_all[0, q]
        for p in range(1, 8):
            value = value + val_all[p, q]
        model_cols.append(jnp.sum(jnp.where(hots[q], value, 0.0), axis=1, keepdims=True))
        residual = wgt_cols[q] * (model_cols[q] - obs_cols[q])
        resids.append(to_col(jnp.sum(jnp.where(hots[q], residual, 0.0), axis=0, keepdims=True)))

    def span_of(c):
        return pl.ds(pl.multiple_of(c * chunk, chunk), chunk)

    def g_up(d, c):
        span = span_of(c)
        return remote(
            send_up.at[d, :, span], recv_up.at[d, :, span], gup_s.at[d, c], gup_r.at[d, c], above
        )

    def g_dn(d, c):
        span = span_of(c)
        return remote(
            send_dn.at[d, :, span], recv_dn.at[d, :, span], gdn_s.at[d, c], gdn_r.at[d, c], below
        )

    def first(c, carry):
        span = span_of(c)
        for q in range(4):
            rows = pl.ds(q * pair, pair)
            contrib[rows, :] = (resids[q] * foot_all[rows, span].astype(jnp.float32)).astype(jnp.bfloat16)
        summed = jnp.dot(pick[...], contrib[...], preferred_element_type=jnp.float32)
        for d in range(depth):
            part[d, :, span] = summed[d * rows_plane : (d + 1) * rows_plane]

        @pl.when(z == 0)
        def _():
            send_up[depth - 1, :, span] = part[depth - 1, :, span].astype(jnp.bfloat16)
            g_up(depth - 1, c).start()

        @pl.when(z == depth - 1)
        def _():
            send_dn[0, :, span] = part[0, :, span].astype(jnp.bfloat16)
            g_dn(0, c).start()

        return carry

    lax.fori_loop(0, CHUNKS, first, 0)

    for s in range(depth - 2, 0, -1):

        def pass_on(c, carry):
            span = span_of(c)

            @pl.when(z + s < depth)
            def _():
                d = z + s

                @pl.when(z > 0)
                def _():
                    g_up(d, c).wait_recv()
                    summed = part[d, :, span] + recv_up[d, :, span].astype(jnp.float32)
                    send_up[d, :, span] = summed.astype(jnp.bfloat16)

                @pl.when(z == 0)
                def _():
                    send_up[d, :, span] = part[d, :, span].astype(jnp.bfloat16)

                g_up(d, c).start()

            @pl.when(z >= s)
            def _():
                d = z - s

                @pl.when(has_up)
                def _():
                    g_dn(d, c).wait_recv()
                    summed = part[d, :, span] + recv_dn[d, :, span].astype(jnp.float32)
                    send_dn[d, :, span] = summed.astype(jnp.bfloat16)

                @pl.when(z == depth - 1)
                def _():
                    send_dn[d, :, span] = part[d, :, span].astype(jnp.bfloat16)

                g_dn(d, c).start()

            return carry

        lax.fori_loop(0, CHUNKS, pass_on, 0)

    def out_copy(k, c):
        rows = pl.ds(pl.multiple_of(place_of(k) * rows_dev, rows_dev), rows_dev)
        into = pl.ds(pl.multiple_of(me * cells + c * chunk, chunk), chunk)
        return remote(
            total.at[rows, span_of(c)], out.at[:, into], out_s.at[k, c], out_r.at[k, c], device(k)
        )

    def finish(c, carry):
        span = span_of(c)
        total[:, span] = part[z, :, span]

        @pl.when(has_down)
        def _():
            g_up(z, c).wait_recv()
            total[:, span] = total[:, span] + recv_up[z, :, span].astype(jnp.float32)

        @pl.when(has_up)
        def _():
            g_dn(z, c).wait_recv()
            total[:, span] = total[:, span] + recv_dn[z, :, span].astype(jnp.float32)

        for k in (6, 7, 2, 4, 3, 5, 1):
            out_copy(k, c).start()
        into = pl.ds(pl.multiple_of(me * cells + c * chunk, chunk), chunk)
        out[:, into] = total[pl.ds(pl.multiple_of(me * rows_dev, rows_dev), rows_dev), span]
        return carry

    lax.fori_loop(0, CHUNKS, finish, 0)

    modeled = jnp.zeros((1, 2 * sounds), jnp.float32)
    for q in range(4):
        modeled = modeled + jnp.where(chip == q, to_row(model_cols[q]), 0.0)
    modeled_out[...] = jnp.where(core == 0, modeled[:, :sounds], modeled[:, sounds:])

    for k in range(1, 8):
        flux_copy(k).wait_send()
        meta_copy(k).wait_send()
        foot_copy(k).wait_send()
        val_copy(k).wait_send()
    for zz in range(depth):
        for q in range(4):
            pl.when(has_up & (zz <= z))(lambda: z_up(zz, q).wait_send())
            pl.when(has_down & (zz >= z))(lambda: z_dn(zz, q).wait_send())

    def drain(c, carry):
        for d in range(depth):
            pl.when(d > z)(lambda: g_up(d, c).wait_send())
            pl.when(d < z)(lambda: g_dn(d, c).wait_send())
        for k in range(1, 8):
            out_copy(k, c).wait()
        return carry

    lax.fori_loop(0, CHUNKS, drain, 0)


def per_plane(depth, flux, footprint, owner, tile, lag, sounding, swin, observed, weight):
    windows, tile_dev, all_cells = flux.shape
    entries = footprint.shape[0]
    cells = all_cells // 8
    rows_dev = windows * tile_dev
    rows_plane = 8 * rows_dev
    rows_all = depth * rows_plane
    sounds = observed.shape[1]
    bf, f32 = jnp.bfloat16, jnp.float32
    vmem, hbm = pl.BlockSpec(memory_space=pltpu.VMEM), pl.BlockSpec(memory_space=pl.ANY)
    dma = pltpu.SemaphoreType.DMA
    modeled, gradient = pl.pallas_call(
        functools.partial(plane_kernel, depth, windows, tile_dev),
        out_shape=(
            jax.ShapeDtypeStruct((1, sounds), f32),
            jax.ShapeDtypeStruct((rows_dev, all_cells), f32),
        ),
        in_specs=[hbm, hbm] + [vmem] * 7,
        out_specs=(vmem, vmem),
        scratch_shapes=[
            pltpu.VMEM((depth, 4, 2, windows, tile_dev, cells), bf),
            pltpu.VMEM((rows_all, cells), bf),
            pltpu.VMEM((8 * entries, cells), bf),
            pltpu.VMEM((8, 8, 2 * entries), f32),
            pltpu.VMEM((8, 4, 1, 2 * entries), f32),
            pltpu.VMEM((rows_all, 8 * entries), bf),
            pltpu.VMEM((8 * entries, cells // CHUNKS), bf),
            pltpu.VMEM((depth, rows_plane, cells), f32),
            *[pltpu.VMEM((depth, rows_plane, cells), bf)] * 4,
            pltpu.VMEM((rows_plane, cells), f32),
            *[dma((8,))] * 6,
            *[dma((depth, 4))] * 4,
            *[dma((8,))] * 2,
            *[dma((depth, CHUNKS))] * 4,
            *[dma((8, CHUNKS))] * 2,
            dma((2,)),
        ],
        compiler_params=pltpu.CompilerParams(collective_id=0, has_side_effects=True),
    )(flux, footprint, owner.reshape(1, entries), tile, lag, sounding, swin, observed, weight)
    return modeled, gradient.reshape(windows, tile_dev, all_cells)


def solution(mesh):
    placed = (
        P("tm", "obs", None),
        P(("tm", "obs"), None),
        P(("tm", "obs"), None),
        P(("tm", "obs"), None),
        P(("tm", "obs"), None),
        P(("tm", "obs"), None),
        P(("tm", "obs"), None),
        P(("tm", "obs"), None),
        P(("tm", "obs"), None),
    )
    times, places = mesh.shape["tm"], mesh.shape["obs"]
    depth = places // 4
    grouped = times == 2 and places % 4 == 0 and depth >= 2

    def routed(flux, *rest):
        rows = flux.shape[0] * flux.shape[1] * times * places
        fits = rows * flux.shape[2] * 5 <= 40 * 2**20
        plain = flux.shape[0] * flux.shape[1] % 8 == 0 and flux.shape[2] % 16384 == 0
        plain = plain and rest[0].shape[0] % 64 == 0
        body = functools.partial(per_plane, depth) if grouped and fits and plain else per_device
        return body(flux, *rest)

    return jax.shard_map(
        routed,
        mesh=mesh,
        in_specs=placed,
        out_specs=(P(("tm", "obs"), None), P("tm", "obs", None)),
        check_vma=False,
    )
```

```python
import functools

import jax
import jax.numpy as jnp
from jax import lax
from jax.experimental import pallas as pl
from jax.experimental.pallas import tpu as pltpu
from jax.sharding import PartitionSpec as P


def per_device(
    flux,
    footprint,
    entry_owner,
    entry_tile,
    entry_lag,
    entry_sounding,
    sounding_window,
    observed,
    obs_weight,
):
    peer_count = lax.axis_size("obs")
    entry_count = footprint.shape[0]
    cell_count = footprint.shape[1]
    tile_dev = flux.shape[1]
    sounding_count = observed.shape[1]
    slot_cap = 2 * entry_count // peer_count
    owners = entry_owner[:, 0]
    sounding = entry_sounding[0]
    sounding_hot = sounding[:, None] == jnp.arange(sounding_count, dtype=jnp.int32)[None, :]
    window = jnp.sum(jnp.where(sounding_hot, sounding_window[0][None, :], 0), axis=1) - entry_lag[0]
    target = window * tile_dev + entry_tile[0]
    owner_hot = (owners[:, None] == jnp.arange(peer_count, dtype=jnp.int32)[None, :]).astype(
        jnp.int32
    )
    rank_within = jnp.sum((jnp.cumsum(owner_hot, axis=0) - owner_hot) * owner_hot, axis=1)
    slot_index = owners * slot_cap + rank_within
    send_blocks = (
        jnp.zeros((peer_count * slot_cap, cell_count), jnp.bfloat16).at[slot_index].set(footprint)
    )
    send_blocks = send_blocks.reshape(peer_count, slot_cap, cell_count)
    send_target = jnp.zeros((peer_count * slot_cap,), jnp.int32).at[slot_index].set(target)
    send_target = send_target.reshape(peer_count, slot_cap)
    everything = lax.all_gather(flux, "tm", axis=0, tiled=True).reshape(-1, cell_count)
    got_blocks, got_target = (
        lax.all_to_all(send_blocks, "obs", split_axis=0, concat_axis=0, tiled=True),
        lax.all_to_all(send_target, "obs", split_axis=0, concat_axis=0, tiled=True),
    )
    selected = everything[got_target.reshape(-1)].reshape(got_blocks.shape)
    returned = lax.all_to_all(
        jnp.einsum("pkc,pkc->pk", got_blocks, selected, preferred_element_type=jnp.float32),
        "obs",
        split_axis=0,
        concat_axis=0,
        tiled=True,
    )
    entry_dots = returned.reshape(-1)[slot_index]
    modeled = jnp.sum(jnp.where(sounding_hot, entry_dots[:, None], 0.0), axis=0)
    residual = obs_weight[0] * (modeled - observed[0])
    entry_resid = jnp.sum(jnp.where(sounding_hot, residual[None, :], 0.0), axis=1)
    slot_resid = jnp.zeros((peer_count * slot_cap,), jnp.float32).at[slot_index].set(entry_resid)
    got_resid = lax.all_to_all(
        slot_resid.reshape(peer_count, slot_cap), "obs", split_axis=0, concat_axis=0, tiled=True
    )
    contribution = (got_resid[:, :, None] * got_blocks).astype(jnp.bfloat16)
    targets = got_target
    contribution = contribution.reshape(-1, cell_count)
    targets = targets.reshape(-1)
    row_count = flux.shape[0] * lax.axis_size("tm")
    row_ids = jnp.arange(row_count * tile_dev, dtype=jnp.int32)
    row_match = (row_ids[:, None] == targets[None, :]).astype(jnp.bfloat16)
    summed = jnp.dot(row_match, contribution, preferred_element_type=jnp.float32)
    gradient = lax.psum_scatter(
        summed.reshape(row_count, tile_dev * cell_count), "tm", scatter_dimension=0, tiled=True
    )
    gradient = gradient.reshape(flux.shape[0], tile_dev, cell_count)
    return (modeled[None, :], gradient)


CHUNKS = 8
FOOT_ORDER = ((1, None), (6, None), (7, None), (2, None), (4, None), (3, 0), (5, 0), (3, 1), (5, 1))


def eye(n):
    return lax.broadcasted_iota(jnp.int32, (n, n), 0) == lax.broadcasted_iota(jnp.int32, (n, n), 1)


def to_col(row):
    return jnp.sum(jnp.where(eye(row.shape[1]), row, 0.0), axis=1, keepdims=True)


def to_row(col):
    return jnp.sum(jnp.where(eye(col.shape[0]), col, 0.0), axis=0, keepdims=True)


def plane_kernel(
    depth, windows, tile_dev, flux, foot, owner_h, tile_h, lag_h, sounding_h, swin_h, observed_h, weight_h,
    modeled_out, out, owner, tile, lag, sounding, swin, observed, weight,
    staged, gath, foot_all, meta_all, val_all, pick, contrib, part, send_up, send_dn, recv_up, recv_dn, total,
    flux_s, flux_r, meta_s, meta_r, foot_s, foot_r, zup_s, zup_r, zdn_s, zdn_r, val_s, val_r,
    gup_s, gup_r, gdn_s, gdn_r, out_s, out_r, local_sem,
):
    entries, all_cells = foot.shape
    cells = all_cells // 8
    rows_dev = windows * tile_dev
    rows_plane = 8 * rows_dev
    rows_all = depth * rows_plane
    sounds = observed.shape[1]
    pair = 2 * entries
    chunk = cells // CHUNKS
    y = lax.axis_index("tm")
    o = lax.axis_index("obs")
    core = lax.rem(o, 2)
    x = lax.rem(o // 2, 2)
    z = o // 4
    chip = y * 2 + x
    me = chip * 2 + core
    has_up = z < depth - 1
    has_down = z > 0
    above = (y, o + 4)
    below = (y, o - 4)

    def peer(k):
        yy = 1 - y if k & 4 else y
        xx = 1 - x if k & 2 else x
        cc = 1 - core if k & 1 else core
        return yy, xx, cc

    def device(k):
        yy, xx, cc = peer(k)
        return (yy, z * 4 + xx * 2 + cc)

    def place_of(k):
        yy, xx, cc = peer(k)
        return (yy * 2 + xx) * 2 + cc

    def chip_of(q):
        yy, xx, _ = peer(2 * q)
        return yy * 2 + xx

    def eighth(k):
        return pl.ds(pl.multiple_of(place_of(k) * cells, cells), cells)

    def remote(src, dst, send, recv, to):
        return pltpu.make_async_remote_copy(
            src_ref=src, dst_ref=dst, send_sem=send, recv_sem=recv,
            device_id=to, device_id_type=pl.DeviceIdType.MESH,
        )

    barrier = pltpu.get_barrier_semaphore()

    def greet(to):
        pl.semaphore_signal(barrier, inc=1, device_id=to, device_id_type=pl.DeviceIdType.MESH)

    for k in range(1, 8):
        greet(device(k))
    pl.when(has_up)(lambda: greet(above))
    pl.when(has_down)(lambda: greet(below))
    own_flux = pltpu.make_async_copy(flux.at[:, :, eighth(0)], staged.at[z, chip, core], local_sem.at[0])
    own_foot = pltpu.make_async_copy(
        foot.at[:, eighth(0)], foot_all.at[pl.ds(pl.multiple_of(me * entries, entries), entries)], local_sem.at[1]
    )
    pairs = (
        (owner_h, owner), (tile_h, tile), (lag_h, lag), (sounding_h, sounding),
        (swin_h, swin), (observed_h, observed), (weight_h, weight),
    )
    small = [
        pltpu.make_async_copy(src, dst, local_sem.at[2 + at]) for at, (src, dst) in enumerate(pairs)
    ]
    for copy in small:
        copy.start()
    own_flux.start()
    own_foot.start()

    pl.semaphore_wait(barrier, 7 + jnp.where(has_up, 1, 0) + jnp.where(has_down, 1, 0))

    def flux_copy(k):
        return remote(
            flux.at[:, :, eighth(k)], staged.at[z, chip, core], flux_s.at[k], flux_r.at[k], device(k)
        )

    def meta_copy(k):
        return remote(meta_all.at[me], meta_all.at[me], meta_s.at[k], meta_r.at[k], device(k))

    def foot_copy(k, half):
        rows = pl.ds(pl.multiple_of(me * entries, entries), entries)
        if half is None:
            return remote(foot.at[:, eighth(k)], foot_all.at[rows], foot_s.at[0, k], foot_r.at[0, k], device(k))
        src = pl.ds(pl.multiple_of(place_of(k) * cells + half * (cells // 2), cells // 2), cells // 2)
        return remote(
            foot.at[:, src], foot_all.at[rows, pl.ds(half * (cells // 2), cells // 2)],
            foot_s.at[half, k], foot_r.at[half, k], device(k),
        )

    def val_copy(k):
        return remote(val_all.at[me], val_all.at[me], val_s.at[k], val_r.at[k], device(k))

    def z_up(zz, q):
        block = staged.at[zz, chip_of(q)]
        return remote(block, block, zup_s.at[zz, q], zup_r.at[zz, q], above)

    def z_dn(zz, q):
        block = staged.at[zz, chip_of(q)]
        return remote(block, block, zdn_s.at[zz, q], zdn_r.at[zz, q], below)

    for k in range(1, 8):
        flux_copy(k).start()
    for copy in small:
        copy.wait()
    hot = lax.broadcasted_iota(jnp.int32, (sounds, entries), 0) == sounding[...]
    window = jnp.sum(
        jnp.where(hot, to_col(swin[...].astype(jnp.float32)), 0.0), axis=0, keepdims=True
    ).astype(jnp.int32) - lag[...]
    own = owner[...]
    late = jnp.where(window >= windows, 1, 0)
    holder = ((own >> 2) * 4 + late * 2 + ((own >> 1) & 1)) * 2 + (own & 1)
    ids = holder * rows_dev + (window - late * windows) * tile_dev + tile[...]
    base = jnp.zeros((1, entries), jnp.float32)
    fill = jnp.zeros((1, pair - sounds), jnp.float32)
    meta_all[me] = jnp.concatenate(
        [
            jnp.concatenate([ids.astype(jnp.float32), base], axis=1),
            jnp.concatenate([(sounding[...] + core * sounds).astype(jnp.float32), base], axis=1),
            jnp.concatenate([observed[...], fill], axis=1),
            jnp.concatenate([weight[...], fill], axis=1),
            jnp.zeros((4, pair), jnp.float32),
        ],
        axis=0,
    )
    for k in range(1, 8):
        meta_copy(k).start()
    for k, half in FOOT_ORDER:
        foot_copy(k, half).start()

    def settle(zz, q):
        at = chip_of(q)
        rows = pl.ds(pl.multiple_of(zz * rows_plane + at * 2 * rows_dev, 2 * rows_dev), 2 * rows_dev)

        def body(step, carry):
            span = pl.ds(pl.multiple_of(step * 512, 512), 512)
            gath[rows, span] = staged[zz, at, :, :, :, span].reshape(2 * rows_dev, 512)
            return carry

        lax.fori_loop(0, cells // 512, body, 0)

    for q in range(4):
        if q == 0:
            own_flux.wait()
        else:
            flux_copy(2 * q).wait_recv()
        flux_copy(2 * q + 1).wait_recv()
        pl.when(has_up)(lambda: z_up(z, q).start())
        pl.when(has_down)(lambda: z_dn(z, q).start())
        settle(z, q)
    for s in range(1, depth):
        for q in range(4):
            @pl.when(z >= s)
            def _():
                z_up(z - s, q).wait_recv()
                pl.when(has_up)(lambda: z_up(z - s, q).start())
                settle(z - s, q)

            @pl.when(z + s < depth)
            def _():
                z_dn(z + s, q).wait_recv()
                pl.when(has_down)(lambda: z_dn(z + s, q).start())
                settle(z + s, q)

    for k in range(1, 8):
        meta_copy(k).wait_recv()
    id_rows, hots, obs_cols, wgt_cols = [], [], [], []
    for q in range(4):
        first, second = meta_all[2 * q], meta_all[2 * q + 1]
        both = [jnp.concatenate([first[r : r + 1, :entries], second[r : r + 1, :entries]], axis=1) for r in (0, 1)]
        id_rows.append(both[0].astype(jnp.int32))
        hots.append(
            lax.broadcasted_iota(jnp.int32, (2 * sounds, pair), 0) == both[1].astype(jnp.int32)
        )
        obs_cols.append(
            to_col(jnp.concatenate([first[2:3, :sounds], second[2:3, :sounds]], axis=1))
        )
        wgt_cols.append(
            to_col(jnp.concatenate([first[3:4, :sounds], second[3:4, :sounds]], axis=1))
        )
        row_at = lax.broadcasted_iota(jnp.int32, (rows_all, pair), 0)
        pick[:, q * pair : (q + 1) * pair] = jnp.where(row_at == id_rows[q], 1.0, 0.0).astype(jnp.bfloat16)

    def ids_of(k):
        return meta_all[place_of(k)][0:1, :entries]

    def rows_of(k):
        return pl.ds(pl.multiple_of(place_of(k) * entries, entries), entries)

    def partial_values(a, b, span):
        acc = lax.dot_general(
            gath[:, span],
            jnp.concatenate([foot_all[rows_of(a), span], foot_all[rows_of(b), span]], axis=0),
            (((1,), (1,)), ((), ())),
            preferred_element_type=jnp.float32,
        )
        wanted = jnp.concatenate([ids_of(a), ids_of(b)], axis=1).astype(jnp.int32)
        row_at = lax.broadcasted_iota(jnp.int32, (rows_all, pair), 0)
        return jnp.sum(jnp.where(row_at == wanted, acc, 0.0), axis=0, keepdims=True)

    def keep_values(a, b, found):
        val_all[me, place_of(a)] = found[:, :entries]
        val_all[me, place_of(b)] = found[:, entries:]

    whole = pl.ds(0, cells)
    for a, b in ((0, 1), (6, 7), (2, 4)):
        for k in (a, b):
            if k:
                foot_copy(k, None).wait_recv()
            else:
                own_foot.wait()
        keep_values(a, b, partial_values(a, b, whole))
    last = jnp.zeros((1, pair), jnp.float32)
    for half in range(2):
        foot_copy(3, half).wait_recv()
        foot_copy(5, half).wait_recv()
        last = last + partial_values(3, 5, pl.ds(half * (cells // 2), cells // 2))
    keep_values(3, 5, last)
    for k in (6, 7, 2, 4, 3, 5, 1):
        val_copy(k).start()
    for k in (1, 2, 3, 4, 5, 6, 7):
        val_copy(k).wait_recv()
    model_cols, resids = [], []
    for q in range(4):
        sums = []
        for b in (2 * q, 2 * q + 1):
            value = val_all[0, b]
            for p in range(1, 8):
                value = value + val_all[p, b]
            sums.append(value)
        value = jnp.concatenate(sums, axis=1)
        model_cols.append(jnp.sum(jnp.where(hots[q], value, 0.0), axis=1, keepdims=True))
        residual = wgt_cols[q] * (model_cols[q] - obs_cols[q])
        resids.append(to_col(jnp.sum(jnp.where(hots[q], residual, 0.0), axis=0, keepdims=True)))

    def span_of(c):
        return pl.ds(pl.multiple_of(c * chunk, chunk), chunk)

    def g_up(d, c):
        span = span_of(c)
        return remote(
            send_up.at[d, :, span], recv_up.at[d, :, span], gup_s.at[d, c], gup_r.at[d, c], above
        )

    def g_dn(d, c):
        span = span_of(c)
        return remote(
            send_dn.at[d, :, span], recv_dn.at[d, :, span], gdn_s.at[d, c], gdn_r.at[d, c], below
        )

    def first(c, carry):
        span = span_of(c)
        for q in range(4):
            rows = pl.ds(q * pair, pair)
            contrib[rows, :] = (resids[q] * foot_all[rows, span].astype(jnp.float32)).astype(jnp.bfloat16)
        summed = jnp.dot(pick[...], contrib[...], preferred_element_type=jnp.float32)
        for d in range(depth):
            part[d, :, span] = summed[d * rows_plane : (d + 1) * rows_plane]

        @pl.when(z == 0)
        def _():
            send_up[depth - 1, :, span] = part[depth - 1, :, span].astype(jnp.bfloat16)
            g_up(depth - 1, c).start()

        @pl.when(z == depth - 1)
        def _():
            send_dn[0, :, span] = part[0, :, span].astype(jnp.bfloat16)
            g_dn(0, c).start()

        return carry

    lax.fori_loop(0, CHUNKS, first, 0)

    for s in range(depth - 2, 0, -1):

        def pass_on(c, carry):
            span = span_of(c)

            @pl.when(z + s < depth)
            def _():
                d = z + s

                @pl.when(z > 0)
                def _():
                    g_up(d, c).wait_recv()
                    summed = part[d, :, span] + recv_up[d, :, span].astype(jnp.float32)
                    send_up[d, :, span] = summed.astype(jnp.bfloat16)

                @pl.when(z == 0)
                def _():
                    send_up[d, :, span] = part[d, :, span].astype(jnp.bfloat16)

                g_up(d, c).start()

            @pl.when(z >= s)
            def _():
                d = z - s

                @pl.when(has_up)
                def _():
                    g_dn(d, c).wait_recv()
                    summed = part[d, :, span] + recv_dn[d, :, span].astype(jnp.float32)
                    send_dn[d, :, span] = summed.astype(jnp.bfloat16)

                @pl.when(z == depth - 1)
                def _():
                    send_dn[d, :, span] = part[d, :, span].astype(jnp.bfloat16)

                g_dn(d, c).start()

            return carry

        lax.fori_loop(0, CHUNKS, pass_on, 0)

    def out_copy(k, c):
        rows = pl.ds(pl.multiple_of(place_of(k) * rows_dev, rows_dev), rows_dev)
        into = pl.ds(pl.multiple_of(me * cells + c * chunk, chunk), chunk)
        return remote(
            total.at[rows, span_of(c)], out.at[:, into], out_s.at[k, c], out_r.at[k, c], device(k)
        )

    def finish(c, carry):
        span = span_of(c)
        total[:, span] = part[z, :, span]

        @pl.when(has_down)
        def _():
            g_up(z, c).wait_recv()
            total[:, span] = total[:, span] + recv_up[z, :, span].astype(jnp.float32)

        @pl.when(has_up)
        def _():
            g_dn(z, c).wait_recv()
            total[:, span] = total[:, span] + recv_dn[z, :, span].astype(jnp.float32)

        for k in (6, 7, 2, 4, 3, 5, 1):
            out_copy(k, c).start()
        into = pl.ds(pl.multiple_of(me * cells + c * chunk, chunk), chunk)
        out[:, into] = total[pl.ds(pl.multiple_of(me * rows_dev, rows_dev), rows_dev), span]
        return carry

    lax.fori_loop(0, CHUNKS, finish, 0)

    modeled = jnp.zeros((1, 2 * sounds), jnp.float32)
    for q in range(4):
        modeled = modeled + jnp.where(chip == q, to_row(model_cols[q]), 0.0)
    modeled_out[...] = jnp.where(core == 0, modeled[:, :sounds], modeled[:, sounds:])

    for k in range(1, 8):
        flux_copy(k).wait_send()
        meta_copy(k).wait_send()
        val_copy(k).wait_send()
    for k, half in FOOT_ORDER:
        foot_copy(k, half).wait_send()
    for zz in range(depth):
        for q in range(4):
            pl.when(has_up & (zz <= z))(lambda: z_up(zz, q).wait_send())
            pl.when(has_down & (zz >= z))(lambda: z_dn(zz, q).wait_send())

    def drain(c, carry):
        for d in range(depth):
            pl.when(d > z)(lambda: g_up(d, c).wait_send())
            pl.when(d < z)(lambda: g_dn(d, c).wait_send())
        for k in range(1, 8):
            out_copy(k, c).wait()
        return carry

    lax.fori_loop(0, CHUNKS, drain, 0)


def deliver(modeled, gradient, modeled_out, gradient_out):
    modeled_out[...] = modeled[...]
    gradient_out[...] = gradient[...].reshape(gradient_out.shape)


def per_plane(depth, flux, footprint, owner, tile, lag, sounding, swin, observed, weight):
    windows, tile_dev, all_cells = flux.shape
    entries = footprint.shape[0]
    cells = all_cells // 8
    rows_dev = windows * tile_dev
    rows_plane = 8 * rows_dev
    rows_all = depth * rows_plane
    sounds = observed.shape[1]
    bf, f32 = jnp.bfloat16, jnp.float32
    vmem, hbm = pl.BlockSpec(memory_space=pltpu.VMEM), pl.BlockSpec(memory_space=pl.ANY)
    dma = pltpu.SemaphoreType.DMA
    modeled, gradient = pl.pallas_call(
        functools.partial(plane_kernel, depth, windows, tile_dev),
        out_shape=(
            jax.ShapeDtypeStruct((1, sounds), f32),
            jax.ShapeDtypeStruct((rows_dev, all_cells), f32),
        ),
        in_specs=[hbm] * 9,
        out_specs=(vmem, vmem),
        scratch_shapes=[
            *[pltpu.VMEM((1, entries), jnp.int32)] * 4,
            pltpu.VMEM((1, sounds), jnp.int32),
            *[pltpu.VMEM((1, sounds), f32)] * 2,
            pltpu.VMEM((depth, 4, 2, windows, tile_dev, cells), bf),
            pltpu.VMEM((rows_all, cells), bf),
            pltpu.VMEM((8 * entries, cells), bf),
            pltpu.VMEM((8, 8, 2 * entries), f32),
            pltpu.VMEM((8, 8, 1, entries), f32),
            pltpu.VMEM((rows_all, 8 * entries), bf),
            pltpu.VMEM((8 * entries, cells // CHUNKS), bf),
            pltpu.VMEM((depth, rows_plane, cells), f32),
            *[pltpu.VMEM((depth, rows_plane, cells), bf)] * 4,
            pltpu.VMEM((rows_plane, cells), f32),
            *[dma((8,))] * 4,
            *[dma((2, 8))] * 2,
            *[dma((depth, 4))] * 4,
            *[dma((8,))] * 2,
            *[dma((depth, CHUNKS))] * 4,
            *[dma((8, CHUNKS))] * 2,
            dma((9,)),
        ],
        compiler_params=pltpu.CompilerParams(collective_id=0, has_side_effects=True),
    )(flux, footprint, owner.reshape(1, entries), tile, lag, sounding, swin, observed, weight)
    return pl.pallas_call(
        deliver,
        out_shape=(
            jax.ShapeDtypeStruct((1, sounds), f32),
            jax.ShapeDtypeStruct((windows, tile_dev, all_cells), f32),
        ),
        in_specs=[vmem] * 2,
        out_specs=(vmem, vmem),
    )(modeled, gradient)


def solution(mesh):
    placed = (
        P("tm", "obs", None),
        P(("tm", "obs"), None),
        P(("tm", "obs"), None),
        P(("tm", "obs"), None),
        P(("tm", "obs"), None),
        P(("tm", "obs"), None),
        P(("tm", "obs"), None),
        P(("tm", "obs"), None),
        P(("tm", "obs"), None),
    )
    times, places = mesh.shape["tm"], mesh.shape["obs"]
    depth = places // 4
    grouped = times == 2 and places % 4 == 0 and depth >= 2

    def routed(flux, *rest):
        rows = flux.shape[0] * flux.shape[1] * times * places
        fits = rows * flux.shape[2] * 5 <= 40 * 2**20
        plain = flux.shape[0] * flux.shape[1] % 8 == 0 and flux.shape[2] % 16384 == 0
        plain = plain and rest[0].shape[0] % 64 == 0
        body = functools.partial(per_plane, depth) if grouped and fits and plain else per_device
        return body(flux, *rest)

    return jax.shard_map(
        routed,
        mesh=mesh,
        in_specs=placed,
        out_specs=(P(("tm", "obs"), None), P("tm", "obs", None)),
        check_vma=False,
    )
```
